32 devices in a mesh: tok: 4 (over x, core), vocab: 8 (over z, y).
Axes of the slice: x: 2, y: 2, z: 4, core: 2. Of those that a mesh axis runs over, the one named last changes fastest.
Arguments:
- hidden_states: bfloat16 [512, 3584], P('tok'), may hold values from -6 to 6, as said below
- hidden_tangent: bfloat16 [512, 3584], P('tok'), may hold values from -6 to 6
- buckets: int32 [512], P('tok'), may hold values from 0 to 7
- head_weight: bfloat16 [3584, 5120], P(None, 'vocab')
Outputs:
- hidden_cotangent: bfloat16 [3584, 512], P('vocab', 'tok')
- weight_gradient: bfloat16 [3584, 5120], P('tok', 'vocab')
The draws below stay inside these ranges and needn't reach their ends.
Inputs may be any that keep to these rules, and one draw needn't show every extreme that they name: `hidden_states`: hidden states of order one.
All inputs are finite; a program needn't handle non-finite values.
Results may differ from the reference program's by a relative error of at most 0.0107.
Values may be sent and summed in bfloat16 or wider, within the bound.
A program may use at most 64 MiB of HBM per device.

```python
import jax
import jax.numpy as jnp
from jax import lax

D = 3584
TOK_DEV = 128
BUCKETS = 8
VOCAB = 5120
TOKENS = 512
N_TOK = 4


def draw_hidden_states(key, part):
    base = jnp.clip(jax.random.normal(key, (TOKENS, D), jnp.float32), -6.0, 6.0)
    return base.astype(jnp.bfloat16)


def draw_head_weight(key, part):
    spread = 3.0 / D ** 0.5
    base = jnp.clip(jax.random.normal(key, (D, VOCAB), jnp.float32), -6.0, 6.0) * spread
    return base.astype(jnp.bfloat16)


def plant(result, key, least, high):
    index_at = [jax.random.randint(jax.random.fold_in(key, axis), (), 0, length) for axis, length in enumerate(result.shape)]
    main_axis = result.shape.index(max(result.shape))
    next_to = index_at[:main_axis] + [(index_at[main_axis] + 1) % result.shape[main_axis]] + index_at[main_axis + 1:]
    return result.at[tuple(index_at)].set(least).at[tuple(next_to)].set(high)


def levels(rng, dims, split, low, high):
    level, own = 1.0, jax.random.fold_in(rng, 6)
    for dim, parts in split:
        heights = jnp.exp(jax.random.uniform(jax.random.fold_in(own, dim), (parts,), jnp.float32, low / len(split), high / len(split)))
        level = level * jnp.repeat(heights, dims[dim] // parts).reshape([-1 if axis == dim else 1 for axis in range(len(dims))])
    return level


def bell_draw(stream_key, dims, width, reach, split=(), kind=jnp.bfloat16):
    factor_of = levels(stream_key, dims, split, -0.22, 0.18) if split else 1.0
    entries = jax.random.normal(stream_key, dims, jnp.float32) * width * factor_of
    return jnp.minimum(jnp.maximum(entries, -reach), reach).astype(kind)


def setup_inputs(seed: int = 0) -> dict:
    splits = jax.random.split(jax.random.key(seed), 5)
    return {
        "hidden_states": draw_hidden_states(jax.random.fold_in(splits[4], 71), 0),
        "hidden_tangent": bell_draw(splits[1], (TOKENS, D), 1.0, 6.0, ((0, 4),)),
        "buckets": plant(jax.random.randint(splits[2], (TOKENS,), 0, BUCKETS), jax.random.fold_in(splits[2], 1), 0, BUCKETS - 1).astype(jnp.int32),
        "head_weight": draw_head_weight(jax.random.fold_in(splits[4], 71), 0),
    }


def reference(hidden_states, hidden_tangent, buckets, head_weight):
    def one_block(carry, index):
        start = (index * TOK_DEV).astype(jnp.int32)
        rows = lax.dynamic_slice_in_dim(hidden_states, start, TOK_DEV, 0)
        tangent_rows = lax.dynamic_slice_in_dim(hidden_tangent, start, TOK_DEV, 0)
        bucket_rows = lax.dynamic_slice_in_dim(buckets, start, TOK_DEV, 0)
        logits = jnp.dot(rows, head_weight, preferred_element_type=jnp.float32)
        tangent = jnp.dot(tangent_rows, head_weight, preferred_element_type=jnp.float32)
        peak = jnp.max(logits, axis=1, keepdims=True)
        expo = jnp.exp(logits - peak)
        probs = expo / jnp.sum(expo, axis=1, keepdims=True)
        mean = jnp.sum(probs * tangent, axis=1, keepdims=True)
        scale = 0.25 * jnp.exp2(bucket_rows.astype(jnp.float32) * (3.0 / (BUCKETS - 1)))
        grads = (scale[:, None] * probs * (tangent - mean)).astype(jnp.bfloat16)
        cotan = lax.dot_general(head_weight, grads, (((1,), (1,)), ((), ())), preferred_element_type=jnp.float32).astype(jnp.bfloat16)
        partial_term = lax.dot_general(rows, grads, (((0,), (0,)), ((), ())), preferred_element_type=jnp.float32).astype(jnp.bfloat16)
        return carry + partial_term.astype(jnp.float32), cotan

    start_total = jnp.zeros((D, VOCAB), jnp.float32)
    total, cotans = lax.scan(one_block, start_total, jnp.arange(N_TOK, dtype=jnp.int32))
    hidden_cotangent = jnp.transpose(cotans, (1, 0, 2)).reshape(D, TOKENS)
    return hidden_cotangent, total.astype(jnp.bfloat16)
```

```python
import functools

import jax
import jax.numpy as jnp
from jax import lax
from jax.experimental import pallas as pl
from jax.experimental.pallas import tpu as pltpu
from jax.sharding import PartitionSpec as P

TOK_DEV = 128
BUCKETS = 8
MESH = pl.DeviceIdType.MESH

N_TOK = 4
N_Z = 4
N_Y = 2
SUB = 2
W_CHUNKS = 7
ORDER = ((3, 2, 1, 0), (3, 2, 0, 1), (0, 1, 3, 2), (0, 1, 2, 3))


def scale_of(buckets):
    return 0.25 * jnp.exp2(buckets.astype(jnp.float32) * (3.0 / (BUCKETS - 1)))


def by_z(z, values):
    out = values[0]
    for i in range(1, len(values)):
        out = jnp.where(z == i, values[i], out)
    return out


def kernel(
    h_ref, t_ref, b_ref, w_ref, cot_ref, wg_ref,
    hh, w, acc, hall, gall, stats, own, ysend, yrecv, zsend, zrecv, wacc, wout,
    load_sem, wload_sem, hs_sem, hr_sem, gs_sem, gr_sem, ss_sem, sr_sem,
    ys_sem, yr_sem, zs_sem, zr_sem, out_sem,
):
    tok, voc = lax.axis_index("tok"), lax.axis_index("vocab")
    x, core = tok // 2, tok % 2
    z, y = voc // N_Y, voc % N_Y
    tokens, width = h_ref.shape
    vocab = w_ref.shape[1]
    rows = hall.shape[2]
    shard = cot_ref.shape[0]
    piece = shard // SUB

    def tok_peer(d):
        return ((x + d // 2) % 2) * 2 + (core + d % 2) % 2

    def voc_peer(d):
        return (voc + d) % (N_Z * N_Y)

    barrier = pltpu.get_barrier_semaphore()
    for d in range(1, N_TOK):
        pl.semaphore_signal(barrier, inc=1, device_id=(tok_peer(d), voc), device_id_type=MESH)
    for d in range(1, N_Z * N_Y):
        pl.semaphore_signal(barrier, inc=1, device_id=(tok, voc_peer(d)), device_id_type=MESH)

    h_load = pltpu.make_async_copy(h_ref, hh.at[pl.ds(0, tokens)], load_sem.at[0])
    t_load = pltpu.make_async_copy(t_ref, hh.at[pl.ds(tokens, tokens)], load_sem.at[1])
    h_load.start()
    t_load.start()
    depth = width // W_CHUNKS
    w_loads = []
    for i in range(W_CHUNKS):
        part = pl.ds(i * depth, depth)
        load = pltpu.make_async_copy(w_ref.at[part], w.at[part], wload_sem.at[i])
        load.start()
        w_loads.append(load)

    def columns_of(device):
        return pl.ds(pl.multiple_of(device * rows, 128), rows)

    mine = pltpu.make_async_copy(h_ref.at[:, columns_of(tok)], hall.at[0], load_sem.at[2])
    mine.start()

    pl.semaphore_wait(barrier, N_TOK - 1 + N_Z * N_Y - 1)

    h_sends = []
    for d in (1, 2, 3):
        send = pltpu.make_async_remote_copy(
            src_ref=h_ref.at[:, columns_of(tok_peer(d))], dst_ref=hall.at[d],
            send_sem=hs_sem.at[d], recv_sem=hr_sem.at[d],
            device_id=(tok_peer(d), voc), device_id_type=MESH,
        )
        send.start()
        h_sends.append(send)

    h_load.wait()
    t_load.wait()
    for i in range(W_CHUNKS):
        w_loads[i].wait()
        part = pl.ds(i * depth, depth)
        term = jnp.dot(hh[:, part], w[part, :], preferred_element_type=jnp.float32)
        if i == 0:
            acc[...] = term
        else:
            acc[...] += term

    logits, tangent = acc[pl.ds(0, tokens), :], acc[pl.ds(tokens, tokens), :]
    peak = jnp.max(logits, axis=1, keepdims=True)
    expo = jnp.exp(logits - peak)
    total = jnp.sum(expo, axis=1, keepdims=True)
    weighted = jnp.sum(expo * tangent, axis=1, keepdims=True)
    acc[pl.ds(0, tokens), :] = expo
    lane = lax.broadcasted_iota(jnp.int32, (tokens, 128), 1)
    table = jnp.where(lane == 0, peak, jnp.where(lane == 1, total, weighted))
    stats[0] = table.T[0:8, :]
    stat_sends = []
    for d in range(1, N_Z * N_Y):
        send = pltpu.make_async_remote_copy(
            src_ref=stats.at[0], dst_ref=stats.at[d],
            send_sem=ss_sem.at[d], recv_sem=sr_sem.at[d],
            device_id=(tok, voc_peer(d)), device_id_type=MESH,
        )
        send.start()
        stat_sends.append(send)
    scale = scale_of(b_ref[...])
    for send in stat_sends:
        send.wait()

    all_stats = stats[...]
    peaks, totals, sums = all_stats[:, 0, :], all_stats[:, 1, :], all_stats[:, 2, :]
    top = jnp.max(peaks, axis=0, keepdims=True)
    shrink = jnp.exp(peaks - top)
    denominator = jnp.sum(totals * shrink, axis=0, keepdims=True)
    mean = jnp.sum(sums * shrink, axis=0, keepdims=True) / denominator
    factor = scale * shrink[0:1, :] / denominator
    line = lax.broadcasted_iota(jnp.int32, (128, tokens), 0)
    back = jnp.where(line == 0, factor, mean).T
    grads = acc[pl.ds(0, tokens), :] * back[:, 0:1] * (acc[pl.ds(tokens, tokens), :] - back[:, 1:2])
    gall[0] = grads.astype(jnp.bfloat16)
    turned = grads.T.astype(jnp.bfloat16)

    g_sends = []
    for d in (1, 2, 3):
        send = pltpu.make_async_remote_copy(
            src_ref=gall.at[0], dst_ref=gall.at[d],
            send_sem=gs_sem.at[d], recv_sem=gr_sem.at[d],
            device_id=(tok_peer(d), voc), device_id_type=MESH,
        )
        send.start()
        g_sends.append(send)

    y_peer = z * N_Y + (1 - y)
    orders = [by_z(z, [o[k] for o in ORDER]) for k in range(N_Z)]

    def cotangent_of(k, side):
        start = pl.multiple_of((orders[k] * N_Y + side) * shard, 16)
        return jnp.dot(w[pl.ds(start, shard), :], turned, preferred_element_type=jnp.float32)

    y_sends = []
    for k in range(N_Z):
        ysend[k] = cotangent_of(k, 1 - y).astype(jnp.bfloat16)
        for s in range(SUB):
            part = pl.ds(s * piece, piece)
            send = pltpu.make_async_remote_copy(
                src_ref=ysend.at[k, part], dst_ref=yrecv.at[k, part],
                send_sem=ys_sem.at[k, s], recv_sem=yr_sem.at[k, s],
                device_id=(tok, y_peer), device_id_type=MESH,
            )
            send.start()
            y_sends.append(send)
    for k in range(N_Z):
        own[k] = cotangent_of(k, y)

    def weight_term(pair):
        h = hall[pl.ds(2 * pair, 2)].reshape(2 * tokens, rows)
        g = gall[pl.ds(2 * pair, 2)].reshape(2 * tokens, vocab)
        return lax.dot_general(h, g, (((0,), (0,)), ((), ())), preferred_element_type=jnp.float32)

    def z_copy(zz, j, s, right):
        part = pl.ds(s * piece, piece)
        to = zz + 1 if right else zz - 1
        return pltpu.make_async_remote_copy(
            src_ref=zsend.at[j, part], dst_ref=zrecv.at[0 if right else 1, j, part],
            send_sem=zs_sem.at[j, s], recv_sem=zr_sem.at[0 if right else 1, j, s],
            device_id=(tok, min(max(to, 0), N_Z - 1) * N_Y + y), device_id_type=MESH,
        )

    def z_step(zz, k, s):
        j = ORDER[zz][k]
        part = pl.ds(s * piece, piece)
        y_sends[k * SUB + s].wait_recv()
        value = own[k, part] + yrecv[k, part].astype(jnp.float32)
        if j >= zz and zz > 0:
            z_copy(zz, j, s, True).wait_recv()
            value = value + zrecv[0, j, part].astype(jnp.float32)
        if j <= zz and zz < N_Z - 1:
            z_copy(zz, j, s, False).wait_recv()
            value = value + zrecv[1, j, part].astype(jnp.float32)
        if j == zz:
            cot_ref[part, :] = value.astype(jnp.bfloat16)
        else:
            zsend[j, part] = value.astype(jnp.bfloat16)
            z_copy(zz, j, s, j > zz).start()

    def z_steps(ks):
        for zz in range(N_Z):
            @pl.when(z == zz)
            def _(zz=zz):
                for k in ks:
                    for s in range(SUB):
                        z_step(zz, k, s)

    mine.wait()
    h_sends[0].wait()
    g_sends[0].wait()
    wacc[...] = weight_term(0)
    z_steps((0, 1, 2))
    for i in (1, 2):
        h_sends[i].wait()
        g_sends[i].wait()
    wout[...] = (wacc[...] + weight_term(1)).astype(jnp.bfloat16)
    out = pltpu.make_async_copy(wout, wg_ref, out_sem)
    out.start()
    z_steps((3,))

    for send in y_sends:
        send.wait_send()
    for zz in range(N_Z):
        @pl.when(z == zz)
        def _(zz=zz):
            for j in range(N_Z):
                if j != zz:
                    for s in range(SUB):
                        z_copy(zz, j, s, j > zz).wait_send()
    out.wait()


def fused(hidden_states, hidden_tangent, buckets, head_weight):
    tokens, width = hidden_states.shape
    vocab = head_weight.shape[1]
    rows, shard = width // N_TOK, width // (N_Z * N_Y)
    bf16, f32 = jnp.bfloat16, jnp.float32
    dma = pltpu.SemaphoreType.DMA
    vmem = pl.BlockSpec(memory_space=pltpu.VMEM)
    hbm = pl.BlockSpec(memory_space=pl.ANY)
    return pl.pallas_call(
        kernel,
        out_shape=(
            jax.ShapeDtypeStruct((shard, tokens), bf16),
            jax.ShapeDtypeStruct((rows, vocab), bf16),
        ),
        in_specs=[hbm, hbm, vmem, hbm],
        out_specs=(vmem, hbm),
        scratch_shapes=[
            pltpu.VMEM((2 * tokens, width), bf16),
            pltpu.VMEM((width, vocab), bf16),
            pltpu.VMEM((2 * tokens, vocab), f32),
            pltpu.VMEM((N_TOK, tokens, rows), bf16),
            pltpu.VMEM((N_TOK, tokens, vocab), bf16),
            pltpu.VMEM((N_Z * N_Y, 8, tokens), f32),
            pltpu.VMEM((N_Z, shard, tokens), f32),
            pltpu.VMEM((N_Z, shard, tokens), bf16),
            pltpu.VMEM((N_Z, shard, tokens), bf16),
            pltpu.VMEM((N_Z, shard, tokens), bf16),
            pltpu.VMEM((2, N_Z, shard, tokens), bf16),
            pltpu.VMEM((rows, vocab), f32),
            pltpu.VMEM((rows, vocab), bf16),
            dma((3,)),
            dma((W_CHUNKS,)),
            dma((N_TOK,)), dma((N_TOK,)), dma((N_TOK,)), dma((N_TOK,)),
            dma((N_Z * N_Y,)), dma((N_Z * N_Y,)),
            dma((N_Z, SUB)), dma((N_Z, SUB)),
            dma((N_Z, SUB)), dma((2, N_Z, SUB)),
            dma,
        ],
        compiler_params=pltpu.CompilerParams(
            collective_id=0, has_side_effects=True, vmem_limit_bytes=48 * 2**20
        ),
    )(hidden_states, hidden_tangent, buckets.reshape(1, tokens), head_weight)


def local(hidden_states, hidden_tangent, buckets, head_weight):
    logits = jnp.dot(hidden_states, head_weight, preferred_element_type=jnp.float32)
    tangent = jnp.dot(hidden_tangent, head_weight, preferred_element_type=jnp.float32)
    peak = lax.pmax(jnp.max(logits, axis=1), "vocab")
    expo = jnp.exp(logits - peak[:, None])
    total = lax.psum(jnp.sum(expo, axis=1), "vocab")
    probs = expo / total[:, None]
    mean = lax.psum(jnp.sum(probs * tangent, axis=1), "vocab")
    scale = scale_of(buckets)
    grads = (scale[:, None] * probs * (tangent - mean[:, None])).astype(jnp.bfloat16)
    width = head_weight.shape[0]
    cotan = lax.psum_scatter(
        lax.dot_general(
            head_weight, grads, (((1,), (1,)), ((), ())), preferred_element_type=jnp.float32
        ),
        "vocab",
        scatter_dimension=0,
        tiled=True,
    )
    hidden_cotangent = cotan.astype(jnp.bfloat16)
    feature_rows = width // lax.axis_size("tok")
    column_start = lax.axis_index("tok") * feature_rows
    pieces = (
        lax.all_gather(hidden_states, "tok", axis=0, tiled=True),
        lax.all_gather(grads, "tok", axis=0, tiled=True),
    )
    columns = lax.dynamic_slice_in_dim(pieces[0], column_start, feature_rows, 1)
    blocks_h = columns.reshape(-1, TOK_DEV, feature_rows)
    blocks_g = pieces[1].reshape(-1, TOK_DEV, pieces[1].shape[1])
    partial_terms = jnp.einsum(
        "kti,ktv->kiv", blocks_h, blocks_g, preferred_element_type=jnp.float32
    ).astype(jnp.bfloat16)
    summed = jnp.sum(partial_terms.astype(jnp.float32), axis=0)
    return (hidden_cotangent, summed.astype(jnp.bfloat16))


def solution(mesh):
    small = mesh.shape["tok"] == N_TOK and mesh.shape["vocab"] == N_Z * N_Y
    return jax.shard_map(
        fused if small else local,
        mesh=mesh,
        in_specs=(P("tok", None), P("tok", None), P("tok"), P(None, "vocab")),
        out_specs=(P("vocab", "tok"), P("tok", "vocab")),
        check_vma=False,
    )
```

```python
import functools

import jax
import jax.numpy as jnp
from jax import lax
from jax.experimental import pallas as pl
from jax.experimental.pallas import tpu as pltpu
from jax.sharding import PartitionSpec as P

TOK_DEV = 128
BUCKETS = 8
MESH = pl.DeviceIdType.MESH

N_TOK = 4
N_Z = 4
N_Y = 2
SUB = 2
W_CHUNKS = 7
ORDER = ((3, 2, 1, 0), (3, 2, 0, 1), (0, 1, 3, 2), (0, 1, 2, 3))


def scale_of(buckets):
    return 0.25 * jnp.exp2(buckets.astype(jnp.float32) * (3.0 / (BUCKETS - 1)))


def by_z(z, values):
    out = values[0]
    for i in range(1, len(values)):
        out = jnp.where(z == i, values[i], out)
    return out


def kernel(
    h_ref, t_ref, b_ref, w_ref, cot_out, wg_out,
    bvec, cot, hh, w, acc, hall, gall, stats, own, ysend, yrecv, zsend, zrecv, wacc, wout,
    load_sem, wload_sem, hs_sem, hr_sem, gs_sem, gr_sem, ss_sem, sr_sem,
    ys_sem, yr_sem, zs_sem, zr_sem, out_sem,
):
    tok, voc = lax.axis_index("tok"), lax.axis_index("vocab")
    x, core = tok // 2, tok % 2
    z, y = voc // N_Y, voc % N_Y
    tokens, width = h_ref.shape
    vocab = w_ref.shape[1]
    rows = hall.shape[2]
    shard = cot.shape[0]
    piece = shard // SUB

    def tok_peer(d):
        return ((x + d // 2) % 2) * 2 + (core + d % 2) % 2

    def voc_peer(d):
        return (voc + d) % (N_Z * N_Y)

    barrier = pltpu.get_barrier_semaphore()
    for d in range(1, N_TOK):
        pl.semaphore_signal(barrier, inc=1, device_id=(tok_peer(d), voc), device_id_type=MESH)
    for d in range(1, N_Z * N_Y):
        pl.semaphore_signal(barrier, inc=1, device_id=(tok, voc_peer(d)), device_id_type=MESH)

    h_load = pltpu.make_async_copy(h_ref, hh.at[pl.ds(0, tokens)], load_sem.at[0])
    t_load = pltpu.make_async_copy(t_ref, hh.at[pl.ds(tokens, tokens)], load_sem.at[1])
    h_load.start()
    t_load.start()
    depth = width // W_CHUNKS
    w_loads = []
    for i in range(W_CHUNKS):
        part = pl.ds(i * depth, depth)
        load = pltpu.make_async_copy(w_ref.at[part], w.at[part], wload_sem.at[i])
        load.start()
        w_loads.append(load)

    def columns_of(device):
        return pl.ds(pl.multiple_of(device * rows, 128), rows)

    mine = pltpu.make_async_copy(h_ref.at[:, columns_of(tok)], hall.at[0], load_sem.at[2])
    mine.start()
    b_load = pltpu.make_async_copy(b_ref, bvec, load_sem.at[3])
    b_load.start()

    pl.semaphore_wait(barrier, N_TOK - 1 + N_Z * N_Y - 1)

    h_sends = []
    for d in (1, 2, 3):
        send = pltpu.make_async_remote_copy(
            src_ref=h_ref.at[:, columns_of(tok_peer(d))], dst_ref=hall.at[d],
            send_sem=hs_sem.at[d], recv_sem=hr_sem.at[d],
            device_id=(tok_peer(d), voc), device_id_type=MESH,
        )
        send.start()
        h_sends.append(send)

    h_load.wait()
    t_load.wait()
    for i in range(W_CHUNKS):
        w_loads[i].wait()
        part = pl.ds(i * depth, depth)
        term = jnp.dot(hh[:, part], w[part, :], preferred_element_type=jnp.float32)
        if i == 0:
            acc[...] = term
        else:
            acc[...] += term

    logits, tangent = acc[pl.ds(0, tokens), :], acc[pl.ds(tokens, tokens), :]
    peak = jnp.max(logits, axis=1, keepdims=True)
    expo = jnp.exp(logits - peak)
    total = jnp.sum(expo, axis=1, keepdims=True)
    weighted = jnp.sum(expo * tangent, axis=1, keepdims=True)
    acc[pl.ds(0, tokens), :] = expo
    lane = lax.broadcasted_iota(jnp.int32, (tokens, 128), 1)
    table = jnp.where(lane == 0, peak, jnp.where(lane == 1, total, weighted))
    stats[0] = table.T[0:8, :]
    stat_sends = []
    for d in range(1, N_Z * N_Y):
        send = pltpu.make_async_remote_copy(
            src_ref=stats.at[0], dst_ref=stats.at[d],
            send_sem=ss_sem.at[d], recv_sem=sr_sem.at[d],
            device_id=(tok, voc_peer(d)), device_id_type=MESH,
        )
        send.start()
        stat_sends.append(send)
    b_load.wait()
    scale = scale_of(bvec[...])
    for send in stat_sends:
        send.wait()

    all_stats = stats[...]
    peaks, totals, sums = all_stats[:, 0, :], all_stats[:, 1, :], all_stats[:, 2, :]
    top = jnp.max(peaks, axis=0, keepdims=True)
    shrink = jnp.exp(peaks - top)
    denominator = jnp.sum(totals * shrink, axis=0, keepdims=True)
    mean = jnp.sum(sums * shrink, axis=0, keepdims=True) / denominator
    factor = scale * shrink[0:1, :] / denominator
    line = lax.broadcasted_iota(jnp.int32, (128, tokens), 0)
    back = jnp.where(line == 0, factor, mean).T
    grads = acc[pl.ds(0, tokens), :] * back[:, 0:1] * (acc[pl.ds(tokens, tokens), :] - back[:, 1:2])
    gall[0] = grads.astype(jnp.bfloat16)
    turned = grads.T.astype(jnp.bfloat16)

    g_sends = []
    for d in (1, 2, 3):
        send = pltpu.make_async_remote_copy(
            src_ref=gall.at[0], dst_ref=gall.at[d],
            send_sem=gs_sem.at[d], recv_sem=gr_sem.at[d],
            device_id=(tok_peer(d), voc), device_id_type=MESH,
        )
        send.start()
        g_sends.append(send)

    y_peer = z * N_Y + (1 - y)
    orders = [by_z(z, [o[k] for o in ORDER]) for k in range(N_Z)]

    def cotangent_of(k, side):
        start = pl.multiple_of((orders[k] * N_Y + side) * shard, 16)
        return jnp.dot(w[pl.ds(start, shard), :], turned, preferred_element_type=jnp.float32)

    y_sends = []
    for k in range(N_Z):
        ysend[k] = cotangent_of(k, 1 - y).astype(jnp.bfloat16)
        for s in range(SUB):
            part = pl.ds(s * piece, piece)
            send = pltpu.make_async_remote_copy(
                src_ref=ysend.at[k, part], dst_ref=yrecv.at[k, part],
                send_sem=ys_sem.at[k, s], recv_sem=yr_sem.at[k, s],
                device_id=(tok, y_peer), device_id_type=MESH,
            )
            send.start()
            y_sends.append(send)
    for k in range(N_Z):
        own[k] = cotangent_of(k, y)

    def weight_term(pair):
        h = hall[pl.ds(2 * pair, 2)].reshape(2 * tokens, rows)
        g = gall[pl.ds(2 * pair, 2)].reshape(2 * tokens, vocab)
        return lax.dot_general(h, g, (((0,), (0,)), ((), ())), preferred_element_type=jnp.float32)

    def z_copy(zz, j, s, right):
        part = pl.ds(s * piece, piece)
        to = zz + 1 if right else zz - 1
        return pltpu.make_async_remote_copy(
            src_ref=zsend.at[j, part], dst_ref=zrecv.at[0 if right else 1, j, part],
            send_sem=zs_sem.at[j, s], recv_sem=zr_sem.at[0 if right else 1, j, s],
            device_id=(tok, min(max(to, 0), N_Z - 1) * N_Y + y), device_id_type=MESH,
        )

    def z_step(zz, k, s):
        j = ORDER[zz][k]
        part = pl.ds(s * piece, piece)
        y_sends[k * SUB + s].wait_recv()
        value = own[k, part] + yrecv[k, part].astype(jnp.float32)
        if j >= zz and zz > 0:
            z_copy(zz, j, s, True).wait_recv()
            value = value + zrecv[0, j, part].astype(jnp.float32)
        if j <= zz and zz < N_Z - 1:
            z_copy(zz, j, s, False).wait_recv()
            value = value + zrecv[1, j, part].astype(jnp.float32)
        if j == zz:
            cot[part, :] = value.astype(jnp.bfloat16)
        else:
            zsend[j, part] = value.astype(jnp.bfloat16)
            z_copy(zz, j, s, j > zz).start()

    def z_steps(ks):
        for zz in range(N_Z):
            @pl.when(z == zz)
            def _(zz=zz):
                for k in ks:
                    for s in range(SUB):
                        z_step(zz, k, s)

    mine.wait()
    h_sends[0].wait()
    g_sends[0].wait()
    wacc[...] = weight_term(0)
    z_steps((0, 1, 2))
    for i in (1, 2):
        h_sends[i].wait()
        g_sends[i].wait()
    wout[...] = (wacc[...] + weight_term(1)).astype(jnp.bfloat16)
    out = pltpu.make_async_copy(wout, wg_out, out_sem.at[0])
    out.start()
    z_steps((3,))
    cot_store = pltpu.make_async_copy(cot, cot_out, out_sem.at[1])
    cot_store.start()

    for send in y_sends:
        send.wait_send()
    for zz in range(N_Z):
        @pl.when(z == zz)
        def _(zz=zz):
            for j in range(N_Z):
                if j != zz:
                    for s in range(SUB):
                        z_copy(zz, j, s, j > zz).wait_send()
    out.wait()
    cot_store.wait()


def fused(hidden_states, hidden_tangent, buckets, head_weight):
    tokens, width = hidden_states.shape
    vocab = head_weight.shape[1]
    rows, shard = width // N_TOK, width // (N_Z * N_Y)
    bf16, f32 = jnp.bfloat16, jnp.float32
    dma = pltpu.SemaphoreType.DMA
    hbm = pl.BlockSpec(memory_space=pltpu.HBM)
    return pl.pallas_call(
        kernel,
        out_shape=(
            jax.ShapeDtypeStruct((shard, tokens), bf16),
            jax.ShapeDtypeStruct((rows, vocab), bf16),
        ),
        in_specs=[hbm, hbm, hbm, hbm],
        out_specs=(hbm, hbm),
        scratch_shapes=[
            pltpu.VMEM((1, tokens), jnp.int32),
            pltpu.VMEM((shard, tokens), bf16),
            pltpu.VMEM((2 * tokens, width), bf16),
            pltpu.VMEM((width, vocab), bf16),
            pltpu.VMEM((2 * tokens, vocab), f32),
            pltpu.VMEM((N_TOK, tokens, rows), bf16),
            pltpu.VMEM((N_TOK, tokens, vocab), bf16),
            pltpu.VMEM((N_Z * N_Y, 8, tokens), f32),
            pltpu.VMEM((N_Z, shard, tokens), f32),
            pltpu.VMEM((N_Z, shard, tokens), bf16),
            pltpu.VMEM((N_Z, shard, tokens), bf16),
            pltpu.VMEM((N_Z, shard, tokens), bf16),
            pltpu.VMEM((2, N_Z, shard, tokens), bf16),
            pltpu.VMEM((rows, vocab), f32),
            pltpu.VMEM((rows, vocab), bf16),
            dma((4,)),
            dma((W_CHUNKS,)),
            dma((N_TOK,)), dma((N_TOK,)), dma((N_TOK,)), dma((N_TOK,)),
            dma((N_Z * N_Y,)), dma((N_Z * N_Y,)),
            dma((N_Z, SUB)), dma((N_Z, SUB)),
            dma((N_Z, SUB)), dma((2, N_Z, SUB)),
            dma((2,)),
        ],
        compiler_params=pltpu.CompilerParams(
            collective_id=0, has_side_effects=True, vmem_limit_bytes=60 * 2**20
        ),
    )(hidden_states, hidden_tangent, buckets.reshape(1, tokens), head_weight)


def local(hidden_states, hidden_tangent, buckets, head_weight):
    logits = jnp.dot(hidden_states, head_weight, preferred_element_type=jnp.float32)
    tangent = jnp.dot(hidden_tangent, head_weight, preferred_element_type=jnp.float32)
    peak = lax.pmax(jnp.max(logits, axis=1), "vocab")
    expo = jnp.exp(logits - peak[:, None])
    total = lax.psum(jnp.sum(expo, axis=1), "vocab")
    probs = expo / total[:, None]
    mean = lax.psum(jnp.sum(probs * tangent, axis=1), "vocab")
    scale = scale_of(buckets)
    grads = (scale[:, None] * probs * (tangent - mean[:, None])).astype(jnp.bfloat16)
    width = head_weight.shape[0]
    cotan = lax.psum_scatter(
        lax.dot_general(
            head_weight, grads, (((1,), (1,)), ((), ())), preferred_element_type=jnp.float32
        ),
        "vocab",
        scatter_dimension=0,
        tiled=True,
    )
    hidden_cotangent = cotan.astype(jnp.bfloat16)
    feature_rows = width // lax.axis_size("tok")
    column_start = lax.axis_index("tok") * feature_rows
    pieces = (
        lax.all_gather(hidden_states, "tok", axis=0, tiled=True),
        lax.all_gather(grads, "tok", axis=0, tiled=True),
    )
    columns = lax.dynamic_slice_in_dim(pieces[0], column_start, feature_rows, 1)
    blocks_h = columns.reshape(-1, TOK_DEV, feature_rows)
    blocks_g = pieces[1].reshape(-1, TOK_DEV, pieces[1].shape[1])
    partial_terms = jnp.einsum(
        "kti,ktv->kiv", blocks_h, blocks_g, preferred_element_type=jnp.float32
    ).astype(jnp.bfloat16)
    summed = jnp.sum(partial_terms.astype(jnp.float32), axis=0)
    return (hidden_cotangent, summed.astype(jnp.bfloat16))


def solution(mesh):
    small = mesh.shape["tok"] == N_TOK and mesh.shape["vocab"] == N_Z * N_Y
    return jax.shard_map(
        fused if small else local,
        mesh=mesh,
        in_specs=(P("tok", None), P("tok", None), P("tok"), P(None, "vocab")),
        out_specs=(P("vocab", "tok"), P("tok", "vocab")),
        check_vma=False,
    )
```

```python
import functools

import jax
import jax.numpy as jnp
from jax import lax
from jax.experimental import pallas as pl
from jax.experimental.pallas import tpu as pltpu
from jax.sharding import PartitionSpec as P

TOK_DEV = 128
BUCKETS = 8
MESH = pl.DeviceIdType.MESH

N_TOK = 4
N_Z = 4
N_Y = 2
SUB = 2
W_CHUNKS = 4
PARTS = 7
ORDER = ((3, 2, 1, 0), (3, 2, 0, 1), (0, 1, 3, 2), (0, 1, 2, 3))


def scale_of(buckets):
    return 0.25 * jnp.exp2(buckets.astype(jnp.float32) * (3.0 / (BUCKETS - 1)))


def by_z(z, values):
    out = values[0]
    for i in range(1, len(values)):
        out = jnp.where(z == i, values[i], out)
    return out


def kernel(
    h_ref, t_ref, b_ref, w_ref, cot_out, wg_out,
    bvec, cot, hh, w, acc, hall, gall, stats, own, ysend, yrecv, zsend, zrecv, wacc, wout,
    load_sem, wload_sem, hs_sem, hr_sem, gs_sem, gr_sem, ss_sem, sr_sem,
    ys_sem, yr_sem, zs_sem, zr_sem, out_sem,
):
    tok, voc = lax.axis_index("tok"), lax.axis_index("vocab")
    x, core = tok // 2, tok % 2
    z, y = voc // N_Y, voc % N_Y
    tokens, width = h_ref.shape
    vocab = w_ref.shape[1]
    rows = hall.shape[2]
    shard = cot.shape[0]
    piece = shard // SUB

    def tok_peer(d):
        return ((x + d // 2) % 2) * 2 + (core + d % 2) % 2

    def voc_peer(d):
        return (voc + d) % (N_Z * N_Y)

    barrier = pltpu.get_barrier_semaphore()
    for d in range(1, N_TOK):
        pl.semaphore_signal(barrier, inc=1, device_id=(tok_peer(d), voc), device_id_type=MESH)
    for d in range(1, N_Z * N_Y):
        pl.semaphore_signal(barrier, inc=1, device_id=(tok, voc_peer(d)), device_id_type=MESH)

    h_load = pltpu.make_async_copy(h_ref, hh.at[pl.ds(0, tokens)], load_sem.at[0])
    t_load = pltpu.make_async_copy(t_ref, hh.at[pl.ds(tokens, tokens)], load_sem.at[1])
    h_load.start()
    t_load.start()
    depth = width // W_CHUNKS
    w_loads = []
    for i in range(W_CHUNKS):
        part = pl.ds(i * depth, depth)
        load = pltpu.make_async_copy(w_ref.at[part], w.at[part], wload_sem.at[i])
        load.start()
        w_loads.append(load)

    def columns_of(device):
        return pl.ds(pl.multiple_of(device * rows, 128), rows)

    mine = pltpu.make_async_copy(h_ref.at[:, columns_of(tok)], hall.at[0], load_sem.at[2])
    mine.start()
    b_load = pltpu.make_async_copy(b_ref, bvec, load_sem.at[3])
    b_load.start()

    h_load.wait()
    t_load.wait()
    for i in range(W_CHUNKS):
        if i == W_CHUNKS // 2:
            pl.semaphore_wait(barrier, N_TOK - 1 + N_Z * N_Y - 1)

            h_sends = []
            for d in (1, 2, 3):
                send = pltpu.make_async_remote_copy(
                    src_ref=h_ref.at[:, columns_of(tok_peer(d))], dst_ref=hall.at[d],
                    send_sem=hs_sem.at[d], recv_sem=hr_sem.at[d],
                    device_id=(tok_peer(d), voc), device_id_type=MESH,
                )
                send.start()
                h_sends.append(send)
        w_loads[i].wait()
        part = pl.ds(i * depth, depth)
        term = jnp.dot(hh[:, part], w[part, :], preferred_element_type=jnp.float32)
        if i == 0:
            acc[...] = term
        else:
            acc[...] += term

    logits, tangent = acc[pl.ds(0, tokens), :], acc[pl.ds(tokens, tokens), :]
    peak = jnp.max(logits, axis=1, keepdims=True)
    expo = jnp.exp(logits - peak)
    total = jnp.sum(expo, axis=1, keepdims=True)
    weighted = jnp.sum(expo * tangent, axis=1, keepdims=True)
    acc[pl.ds(0, tokens), :] = expo
    lane = lax.broadcasted_iota(jnp.int32, (tokens, 128), 1)
    table = jnp.where(lane == 0, peak, jnp.where(lane == 1, total, weighted))
    stats[0] = table.T[0:8, :]
    stat_sends = []
    for d in range(1, N_Z * N_Y):
        send = pltpu.make_async_remote_copy(
            src_ref=stats.at[0], dst_ref=stats.at[d],
            send_sem=ss_sem.at[d], recv_sem=sr_sem.at[d],
            device_id=(tok, voc_peer(d)), device_id_type=MESH,
        )
        send.start()
        stat_sends.append(send)
    b_load.wait()
    scale = scale_of(bvec[...])
    for send in stat_sends:
        send.wait()

    all_stats = stats[...]
    peaks, totals, sums = all_stats[:, 0, :], all_stats[:, 1, :], all_stats[:, 2, :]
    top = jnp.max(peaks, axis=0, keepdims=True)
    shrink = jnp.exp(peaks - top)
    denominator = jnp.sum(totals * shrink, axis=0, keepdims=True)
    mean = jnp.sum(sums * shrink, axis=0, keepdims=True) / denominator
    factor = scale * shrink[0:1, :] / denominator
    line = lax.broadcasted_iota(jnp.int32, (128, tokens), 0)
    back = jnp.where(line == 0, factor, mean).T
    grads = acc[pl.ds(0, tokens), :] * back[:, 0:1] * (acc[pl.ds(tokens, tokens), :] - back[:, 1:2])
    gall[0] = grads.astype(jnp.bfloat16)
    turned = grads.T.astype(jnp.bfloat16)

    g_sends = []
    for d in (1, 2, 3):
        send = pltpu.make_async_remote_copy(
            src_ref=gall.at[0], dst_ref=gall.at[d],
            send_sem=gs_sem.at[d], recv_sem=gr_sem.at[d],
            device_id=(tok_peer(d), voc), device_id_type=MESH,
        )
        send.start()
        g_sends.append(send)

    y_peer = z * N_Y + (1 - y)
    orders = [by_z(z, [o[k] for o in ORDER]) for k in range(N_Z)]

    def cotangent_of(k, side):
        start = pl.multiple_of((orders[k] * N_Y + side) * shard, 16)
        return jnp.dot(w[pl.ds(start, shard), :], turned, preferred_element_type=jnp.float32)

    y_sends = []
    for k in range(N_Z):
        ysend[k] = cotangent_of(k, 1 - y).astype(jnp.bfloat16)
        for s in range(SUB):
            part = pl.ds(s * piece, piece)
            send = pltpu.make_async_remote_copy(
                src_ref=ysend.at[k, part], dst_ref=yrecv.at[k, part],
                send_sem=ys_sem.at[k, s], recv_sem=yr_sem.at[k, s],
                device_id=(tok, y_peer), device_id_type=MESH,
            )
            send.start()
            y_sends.append(send)
    for k in range(N_Z):
        own[k] = cotangent_of(k, y)

    def weight_term(pair):
        h = hall[pl.ds(2 * pair, 2)].reshape(2 * tokens, rows)
        g = gall[pl.ds(2 * pair, 2)].reshape(2 * tokens, vocab)
        return lax.dot_general(h, g, (((0,), (0,)), ((), ())), preferred_element_type=jnp.float32)

    def z_copy(zz, j, s, right):
        part = pl.ds(s * piece, piece)
        to = zz + 1 if right else zz - 1
        return pltpu.make_async_remote_copy(
            src_ref=zsend.at[j, part], dst_ref=zrecv.at[0 if right else 1, j, part],
            send_sem=zs_sem.at[j, s], recv_sem=zr_sem.at[0 if right else 1, j, s],
            device_id=(tok, min(max(to, 0), N_Z - 1) * N_Y + y), device_id_type=MESH,
        )

    def z_step(zz, k, s):
        j = ORDER[zz][k]
        part = pl.ds(s * piece, piece)
        y_sends[k * SUB + s].wait_recv()
        value = own[k, part] + yrecv[k, part].astype(jnp.float32)
        if j >= zz and zz > 0:
            z_copy(zz, j, s, True).wait_recv()
            value = value + zrecv[0, j, part].astype(jnp.float32)
        if j <= zz and zz < N_Z - 1:
            z_copy(zz, j, s, False).wait_recv()
            value = value + zrecv[1, j, part].astype(jnp.float32)
        if j == zz:
            cot[part, :] = value.astype(jnp.bfloat16)
        else:
            zsend[j, part] = value.astype(jnp.bfloat16)
            z_copy(zz, j, s, j > zz).start()

    def z_steps(ks):
        for zz in range(N_Z):
            @pl.when(z == zz)
            def _(zz=zz):
                for k in ks:
                    for s in range(SUB):
                        z_step(zz, k, s)

    mine.wait()
    h_sends[0].wait()
    g_sends[0].wait()
    wacc[...] = weight_term(0)
    z_steps((0, 1, 2))
    for i in (1, 2):
        h_sends[i].wait()
        g_sends[i].wait()
    wout[...] = (wacc[...] + weight_term(1)).astype(jnp.bfloat16)
    out = pltpu.make_async_copy(wout, wg_out, out_sem.at[0])
    out.start()
    z_steps((3,))
    cot_store = pltpu.make_async_copy(cot, cot_out, out_sem.at[1])
    cot_store.start()

    for send in y_sends:
        send.wait_send()
    for zz in range(N_Z):
        @pl.when(z == zz)
        def _(zz=zz):
            for j in range(N_Z):
                if j != zz:
                    for s in range(SUB):
                        z_copy(zz, j, s, j > zz).wait_send()
    out.wait()
    cot_store.wait()


def store(cot, wg, cot_out, wg_out, cot_held, wg_held, in_sem, out_sem):
    part = wg.shape[0] // PARTS
    moves = [(cot, cot_held, cot_out)]
    for i in range(PARTS):
        at = pl.ds(i * part, part)
        moves.append((wg.at[at], wg_held.at[at], wg_out.at[at]))
    loads = [pltpu.make_async_copy(a, b, in_sem.at[i]) for i, (a, b, _) in enumerate(moves)]
    saves = [pltpu.make_async_copy(b, c, out_sem.at[i]) for i, (_, b, c) in enumerate(moves)]
    for load in loads:
        load.start()
    for load, save in zip(loads, saves):
        load.wait()
        save.start()
    for save in saves:
        save.wait()


def fused(hidden_states, hidden_tangent, buckets, head_weight):
    tokens, width = hidden_states.shape
    vocab = head_weight.shape[1]
    rows, shard = width // N_TOK, width // (N_Z * N_Y)
    bf16, f32 = jnp.bfloat16, jnp.float32
    dma = pltpu.SemaphoreType.DMA
    hbm = pl.BlockSpec(memory_space=pltpu.HBM)
    results = pl.pallas_call(
        kernel,
        out_shape=(
            jax.ShapeDtypeStruct((shard, tokens), bf16),
            jax.ShapeDtypeStruct((rows, vocab), bf16),
        ),
        in_specs=[hbm, hbm, hbm, hbm],
        out_specs=(hbm, hbm),
        scratch_shapes=[
            pltpu.VMEM((1, tokens), jnp.int32),
            pltpu.VMEM((shard, tokens), bf16),
            pltpu.VMEM((2 * tokens, width), bf16),
            pltpu.VMEM((width, vocab), bf16),
            pltpu.VMEM((2 * tokens, vocab), f32),
            pltpu.VMEM((N_TOK, tokens, rows), bf16),
            pltpu.VMEM((N_TOK, tokens, vocab), bf16),
            pltpu.VMEM((N_Z * N_Y, 8, tokens), f32),
            pltpu.VMEM((N_Z, shard, tokens), f32),
            pltpu.VMEM((N_Z, shard, tokens), bf16),
            pltpu.VMEM((N_Z, shard, tokens), bf16),
            pltpu.VMEM((N_Z, shard, tokens), bf16),
            pltpu.VMEM((2, N_Z, shard, tokens), bf16),
            pltpu.VMEM((rows, vocab), f32),
            pltpu.VMEM((rows, vocab), bf16),
            dma((4,)),
            dma((W_CHUNKS,)),
            dma((N_TOK,)), dma((N_TOK,)), dma((N_TOK,)), dma((N_TOK,)),
            dma((N_Z * N_Y,)), dma((N_Z * N_Y,)),
            dma((N_Z, SUB)), dma((N_Z, SUB)),
            dma((N_Z, SUB)), dma((2, N_Z, SUB)),
            dma((2,)),
        ],
        compiler_params=pltpu.CompilerParams(
            collective_id=0, has_side_effects=True, vmem_limit_bytes=60 * 2**20
        ),
    )(hidden_states, hidden_tangent, buckets.reshape(1, tokens), head_weight)
    return pl.pallas_call(
        store,
        out_shape=tuple(jax.ShapeDtypeStruct(r.shape, bf16) for r in results),
        in_specs=[hbm, hbm],
        out_specs=(hbm, hbm),
        scratch_shapes=[
            pltpu.VMEM((shard, tokens), bf16), pltpu.VMEM((rows, vocab), bf16),
            dma((PARTS + 1,)), dma((PARTS + 1,)),
        ],
        compiler_params=pltpu.CompilerParams(vmem_limit_bytes=60 * 2**20),
    )(*results)


def local(hidden_states, hidden_tangent, buckets, head_weight):
    logits = jnp.dot(hidden_states, head_weight, preferred_element_type=jnp.float32)
    tangent = jnp.dot(hidden_tangent, head_weight, preferred_element_type=jnp.float32)
    peak = lax.pmax(jnp.max(logits, axis=1), "vocab")
    expo = jnp.exp(logits - peak[:, None])
    total = lax.psum(jnp.sum(expo, axis=1), "vocab")
    probs = expo / total[:, None]
    mean = lax.psum(jnp.sum(probs * tangent, axis=1), "vocab")
    scale = scale_of(buckets)
    grads = (scale[:, None] * probs * (tangent - mean[:, None])).astype(jnp.bfloat16)
    width = head_weight.shape[0]
    cotan = lax.psum_scatter(
        lax.dot_general(
            head_weight, grads, (((1,), (1,)), ((), ())), preferred_element_type=jnp.float32
        ),
        "vocab",
        scatter_dimension=0,
        tiled=True,
    )
    hidden_cotangent = cotan.astype(jnp.bfloat16)
    feature_rows = width // lax.axis_size("tok")
    column_start = lax.axis_index("tok") * feature_rows
    pieces = (
        lax.all_gather(hidden_states, "tok", axis=0, tiled=True),
        lax.all_gather(grads, "tok", axis=0, tiled=True),
    )
    columns = lax.dynamic_slice_in_dim(pieces[0], column_start, feature_rows, 1)
    blocks_h = columns.reshape(-1, TOK_DEV, feature_rows)
    blocks_g = pieces[1].reshape(-1, TOK_DEV, pieces[1].shape[1])
    partial_terms = jnp.einsum(
        "kti,ktv->kiv", blocks_h, blocks_g, preferred_element_type=jnp.float32
    ).astype(jnp.bfloat16)
    summed = jnp.sum(partial_terms.astype(jnp.float32), axis=0)
    return (hidden_cotangent, summed.astype(jnp.bfloat16))


def solution(mesh):
    small = mesh.shape["tok"] == N_TOK and mesh.shape["vocab"] == N_Z * N_Y
    return jax.shard_map(
        fused if small else local,
        mesh=mesh,
        in_specs=(P("tok", None), P("tok", None), P("tok"), P(None, "vocab")),
        out_specs=(P("vocab", "tok"), P("tok", "vocab")),
        check_vma=False,
    )
```

```python
import functools

import jax
import jax.numpy as jnp
from jax import lax
from jax.experimental import pallas as pl
from jax.experimental.pallas import tpu as pltpu
from jax.sharding import PartitionSpec as P

TOK_DEV = 128
BUCKETS = 8
MESH = pl.DeviceIdType.MESH

N_TOK = 4
N_Z = 4
N_Y = 2
SUB = 4
W_CHUNKS = 4
PARTS = 7
ORDER = ((3, 2, 1, 0), (3, 2, 0, 1), (0, 1, 3, 2), (0, 1, 2, 3))


def scale_of(buckets):
    return 0.25 * jnp.exp2(buckets.astype(jnp.float32) * (3.0 / (BUCKETS - 1)))


def by_z(z, values):
    out = values[0]
    for i in range(1, len(values)):
        out = jnp.where(z == i, values[i], out)
    return out


def kernel(
    h_ref, t_ref, b_ref, w_ref, cot_out, wg_out,
    bvec, cot, hh, w, acc, hall, gall, stats, own, ysend, yrecv, zsend, zrecv, wacc, wout,
    load_sem, wload_sem, hs_sem, hr_sem, gs_sem, gr_sem, ss_sem, sr_sem,
    ys_sem, yr_sem, zs_sem, zr_sem, out_sem,
):
    tok, voc = lax.axis_index("tok"), lax.axis_index("vocab")
    x, core = tok // 2, tok % 2
    z, y = voc // N_Y, voc % N_Y
    tokens, width = h_ref.shape
    vocab = w_ref.shape[1]
    rows = hall.shape[2]
    shard = cot.shape[0]
    piece = shard // SUB

    def tok_peer(d):
        return ((x + d // 2) % 2) * 2 + (core + d % 2) % 2

    def voc_peer(d):
        return (voc + d) % (N_Z * N_Y)

    barrier = pltpu.get_barrier_semaphore()
    for d in range(1, N_TOK):
        pl.semaphore_signal(barrier, inc=1, device_id=(tok_peer(d), voc), device_id_type=MESH)
    for d in range(1, N_Z * N_Y):
        pl.semaphore_signal(barrier, inc=1, device_id=(tok, voc_peer(d)), device_id_type=MESH)

    h_load = pltpu.make_async_copy(h_ref, hh.at[pl.ds(0, tokens)], load_sem.at[0])
    t_load = pltpu.make_async_copy(t_ref, hh.at[pl.ds(tokens, tokens)], load_sem.at[1])
    h_load.start()
    t_load.start()
    depth = width // W_CHUNKS
    w_loads = []
    for i in range(W_CHUNKS):
        part = pl.ds(i * depth, depth)
        load = pltpu.make_async_copy(w_ref.at[part], w.at[part], wload_sem.at[i])
        load.start()
        w_loads.append(load)

    def columns_of(device):
        return pl.ds(pl.multiple_of(device * rows, 128), rows)

    mine = pltpu.make_async_copy(h_ref.at[:, columns_of(tok)], hall.at[0], load_sem.at[2])
    mine.start()
    b_load = pltpu.make_async_copy(b_ref, bvec, load_sem.at[3])
    b_load.start()

    h_load.wait()
    t_load.wait()
    for i in range(W_CHUNKS):
        if i == W_CHUNKS // 2:
            pl.semaphore_wait(barrier, N_TOK - 1 + N_Z * N_Y - 1)

            h_sends = []
            for d in (1, 2, 3):
                send = pltpu.make_async_remote_copy(
                    src_ref=h_ref.at[:, columns_of(tok_peer(d))], dst_ref=hall.at[d],
                    send_sem=hs_sem.at[d], recv_sem=hr_sem.at[d],
                    device_id=(tok_peer(d), voc), device_id_type=MESH,
                )
                send.start()
                h_sends.append(send)
        w_loads[i].wait()
        part = pl.ds(i * depth, depth)
        term = jnp.dot(hh[:, part], w[part, :], preferred_element_type=jnp.float32)
        if i == 0:
            acc[...] = term
        else:
            acc[...] += term

    logits, tangent = acc[pl.ds(0, tokens), :], acc[pl.ds(tokens, tokens), :]
    peak = jnp.max(logits, axis=1, keepdims=True)
    expo = jnp.exp(logits - peak)
    total = jnp.sum(expo, axis=1, keepdims=True)
    weighted = jnp.sum(expo * tangent, axis=1, keepdims=True)
    acc[pl.ds(0, tokens), :] = expo
    lane = lax.broadcasted_iota(jnp.int32, (tokens, 128), 1)
    table = jnp.where(lane == 0, peak, jnp.where(lane == 1, total, weighted))
    stats[0] = table.T[0:8, :]
    stat_sends = []
    for d in range(1, N_Z * N_Y):
        send = pltpu.make_async_remote_copy(
            src_ref=stats.at[0], dst_ref=stats.at[d],
            send_sem=ss_sem.at[d], recv_sem=sr_sem.at[d],
            device_id=(tok, voc_peer(d)), device_id_type=MESH,
        )
        send.start()
        stat_sends.append(send)
    b_load.wait()
    scale = scale_of(bvec[...])
    for send in stat_sends:
        send.wait()

    all_stats = stats[...]
    peaks, totals, sums = all_stats[:, 0, :], all_stats[:, 1, :], all_stats[:, 2, :]
    top = jnp.max(peaks, axis=0, keepdims=True)
    shrink = jnp.exp(peaks - top)
    denominator = jnp.sum(totals * shrink, axis=0, keepdims=True)
    mean = jnp.sum(sums * shrink, axis=0, keepdims=True) / denominator
    factor = scale * shrink[0:1, :] / denominator
    line = lax.broadcasted_iota(jnp.int32, (128, tokens), 0)
    back = jnp.where(line == 0, factor, mean).T
    grads = acc[pl.ds(0, tokens), :] * back[:, 0:1] * (acc[pl.ds(tokens, tokens), :] - back[:, 1:2])
    gall[0] = grads.astype(jnp.bfloat16)
    turned = grads.T.astype(jnp.bfloat16)

    g_sends = []
    for d in (1, 2, 3):
        send = pltpu.make_async_remote_copy(
            src_ref=gall.at[0], dst_ref=gall.at[d],
            send_sem=gs_sem.at[d], recv_sem=gr_sem.at[d],
            device_id=(tok_peer(d), voc), device_id_type=MESH,
        )
        send.start()
        g_sends.append(send)

    y_peer = z * N_Y + (1 - y)
    orders = [by_z(z, [o[k] for o in ORDER]) for k in range(N_Z)]

    def cotangent_of(k, side):
        start = pl.multiple_of((orders[k] * N_Y + side) * shard, 16)
        return jnp.dot(w[pl.ds(start, shard), :], turned, preferred_element_type=jnp.float32)

    y_sends = []
    for k in range(N_Z):
        ysend[k] = cotangent_of(k, 1 - y).astype(jnp.bfloat16)
        for s in range(SUB):
            part = pl.ds(s * piece, piece)
            send = pltpu.make_async_remote_copy(
                src_ref=ysend.at[k, part], dst_ref=yrecv.at[k, part],
                send_sem=ys_sem.at[k, s], recv_sem=yr_sem.at[k, s],
                device_id=(tok, y_peer), device_id_type=MESH,
            )
            send.start()
            y_sends.append(send)
    for k in range(N_Z):
        own[k] = cotangent_of(k, y)

    def weight_term(pair):
        h = hall[pl.ds(2 * pair, 2)].reshape(2 * tokens, rows)
        g = gall[pl.ds(2 * pair, 2)].reshape(2 * tokens, vocab)
        return lax.dot_general(h, g, (((0,), (0,)), ((), ())), preferred_element_type=jnp.float32)

    def z_copy(zz, j, s, right):
        part = pl.ds(s * piece, piece)
        to = zz + 1 if right else zz - 1
        return pltpu.make_async_remote_copy(
            src_ref=zsend.at[j, part], dst_ref=zrecv.at[0 if right else 1, j, part],
            send_sem=zs_sem.at[j, s], recv_sem=zr_sem.at[0 if right else 1, j, s],
            device_id=(tok, min(max(to, 0), N_Z - 1) * N_Y + y), device_id_type=MESH,
        )

    def z_step(zz, k, s):
        j = ORDER[zz][k]
        part = pl.ds(s * piece, piece)
        y_sends[k * SUB + s].wait_recv()
        value = own[k, part] + yrecv[k, part].astype(jnp.float32)
        if j >= zz and zz > 0:
            z_copy(zz, j, s, True).wait_recv()
            value = value + zrecv[0, j, part].astype(jnp.float32)
        if j <= zz and zz < N_Z - 1:
            z_copy(zz, j, s, False).wait_recv()
            value = value + zrecv[1, j, part].astype(jnp.float32)
        if j == zz:
            cot[part, :] = value.astype(jnp.bfloat16)
        else:
            zsend[j, part] = value.astype(jnp.bfloat16)
            z_copy(zz, j, s, j > zz).start()

    def z_steps(ks):
        for zz in range(N_Z):
            @pl.when(z == zz)
            def _(zz=zz):
                for k in ks:
                    for s in range(SUB):
                        z_step(zz, k, s)

    mine.wait()
    h_sends[0].wait()
    g_sends[0].wait()
    wacc[...] = weight_term(0)
    z_steps((0, 1, 2))
    for i in (1, 2):
        h_sends[i].wait()
        g_sends[i].wait()
    wout[...] = (wacc[...] + weight_term(1)).astype(jnp.bfloat16)
    out = pltpu.make_async_copy(wout, wg_out, out_sem.at[0])
    out.start()
    z_steps((3,))
    cot_store = pltpu.make_async_copy(cot, cot_out, out_sem.at[1])
    cot_store.start()

    for send in y_sends:
        send.wait_send()
    for zz in range(N_Z):
        @pl.when(z == zz)
        def _(zz=zz):
            for j in range(N_Z):
                if j != zz:
                    for s in range(SUB):
                        z_copy(zz, j, s, j > zz).wait_send()
    out.wait()
    cot_store.wait()


def store(cot, wg, cot_out, wg_out, cot_held, wg_held, in_sem, out_sem):
    part = wg.shape[0] // PARTS
    moves = [(cot, cot_held, cot_out)]
    for i in range(PARTS):
        at = pl.ds(i * part, part)
        moves.append((wg.at[at], wg_held.at[at], wg_out.at[at]))
    loads = [pltpu.make_async_copy(a, b, in_sem.at[i]) for i, (a, b, _) in enumerate(moves)]
    saves = [pltpu.make_async_copy(b, c, out_sem.at[i]) for i, (_, b, c) in enumerate(moves)]
    for load in loads:
        load.start()
    for load, save in zip(loads, saves):
        load.wait()
        save.start()
    for save in saves:
        save.wait()


def fused(hidden_states, hidden_tangent, buckets, head_weight):
    tokens, width = hidden_states.shape
    vocab = head_weight.shape[1]
    rows, shard = width // N_TOK, width // (N_Z * N_Y)
    bf16, f32 = jnp.bfloat16, jnp.float32
    dma = pltpu.SemaphoreType.DMA
    hbm = pl.BlockSpec(memory_space=pltpu.HBM)
    results = pl.pallas_call(
        kernel,
        out_shape=(
            jax.ShapeDtypeStruct((shard, tokens), bf16),
            jax.ShapeDtypeStruct((rows, vocab), bf16),
        ),
        in_specs=[hbm, hbm, hbm, hbm],
        out_specs=(hbm, hbm),
        scratch_shapes=[
            pltpu.VMEM((1, tokens), jnp.int32),
            pltpu.VMEM((shard, tokens), bf16),
            pltpu.VMEM((2 * tokens, width), bf16),
            pltpu.VMEM((width, vocab), bf16),
            pltpu.VMEM((2 * tokens, vocab), f32),
            pltpu.VMEM((N_TOK, tokens, rows), bf16),
            pltpu.VMEM((N_TOK, tokens, vocab), bf16),
            pltpu.VMEM((N_Z * N_Y, 8, tokens), f32),
            pltpu.VMEM((N_Z, shard, tokens), f32),
            pltpu.VMEM((N_Z, shard, tokens), bf16),
            pltpu.VMEM((N_Z, shard, tokens), bf16),
            pltpu.VMEM((N_Z, shard, tokens), bf16),
            pltpu.VMEM((2, N_Z, shard, tokens), bf16),
            pltpu.VMEM((rows, vocab), f32),
            pltpu.VMEM((rows, vocab), bf16),
            dma((4,)),
            dma((W_CHUNKS,)),
            dma((N_TOK,)), dma((N_TOK,)), dma((N_TOK,)), dma((N_TOK,)),
            dma((N_Z * N_Y,)), dma((N_Z * N_Y,)),
            dma((N_Z, SUB)), dma((N_Z, SUB)),
            dma((N_Z, SUB)), dma((2, N_Z, SUB)),
            dma((2,)),
        ],
        compiler_params=pltpu.CompilerParams(
            collective_id=0, has_side_effects=True, vmem_limit_bytes=60 * 2**20
        ),
    )(hidden_states, hidden_tangent, buckets.reshape(1, tokens), head_weight)
    return pl.pallas_call(
        store,
        out_shape=tuple(jax.ShapeDtypeStruct(r.shape, bf16) for r in results),
        in_specs=[hbm, hbm],
        out_specs=(hbm, hbm),
        scratch_shapes=[
            pltpu.VMEM((shard, tokens), bf16), pltpu.VMEM((rows, vocab), bf16),
            dma((PARTS + 1,)), dma((PARTS + 1,)),
        ],
        compiler_params=pltpu.CompilerParams(vmem_limit_bytes=60 * 2**20),
    )(*results)


def local(hidden_states, hidden_tangent, buckets, head_weight):
    logits = jnp.dot(hidden_states, head_weight, preferred_element_type=jnp.float32)
    tangent = jnp.dot(hidden_tangent, head_weight, preferred_element_type=jnp.float32)
    peak = lax.pmax(jnp.max(logits, axis=1), "vocab")
    expo = jnp.exp(logits - peak[:, None])
    total = lax.psum(jnp.sum(expo, axis=1), "vocab")
    probs = expo / total[:, None]
    mean = lax.psum(jnp.sum(probs * tangent, axis=1), "vocab")
    scale = scale_of(buckets)
    grads = (scale[:, None] * probs * (tangent - mean[:, None])).astype(jnp.bfloat16)
    width = head_weight.shape[0]
    cotan = lax.psum_scatter(
        lax.dot_general(
            head_weight, grads, (((1,), (1,)), ((), ())), preferred_element_type=jnp.float32
        ),
        "vocab",
        scatter_dimension=0,
        tiled=True,
    )
    hidden_cotangent = cotan.astype(jnp.bfloat16)
    feature_rows = width // lax.axis_size("tok")
    column_start = lax.axis_index("tok") * feature_rows
    pieces = (
        lax.all_gather(hidden_states, "tok", axis=0, tiled=True),
        lax.all_gather(grads, "tok", axis=0, tiled=True),
    )
    columns = lax.dynamic_slice_in_dim(pieces[0], column_start, feature_rows, 1)
    blocks_h = columns.reshape(-1, TOK_DEV, feature_rows)
    blocks_g = pieces[1].reshape(-1, TOK_DEV, pieces[1].shape[1])
    partial_terms = jnp.einsum(
        "kti,ktv->kiv", blocks_h, blocks_g, preferred_element_type=jnp.float32
    ).astype(jnp.bfloat16)
    summed = jnp.sum(partial_terms.astype(jnp.float32), axis=0)
    return (hidden_cotangent, summed.astype(jnp.bfloat16))


def solution(mesh):
    small = mesh.shape["tok"] == N_TOK and mesh.shape["vocab"] == N_Z * N_Y
    return jax.shard_map(
        fused if small else local,
        mesh=mesh,
        in_specs=(P("tok", None), P("tok", None), P("tok"), P(None, "vocab")),
        out_specs=(P("vocab", "tok"), P("tok", "vocab")),
        check_vma=False,
    )
```
